32 devices in a mesh: rep: 2 (over y), cp: 4 (over z), tp: 4 (over x, core).
Axes of the slice: x: 2, y: 2, z: 4, core: 2. Of those that a mesh axis runs over, the one named last changes fastest.
Arguments:
- queries: bfloat16 [2048, 8192], P(('rep', 'cp'), 'tp'), parts along dimension 0, may hold values from -16 to 16
- keys: bfloat16 [2048, 1024], P(('rep', 'cp'), 'tp'), parts along dimension 0, may hold values from -16 to 16
- values: bfloat16 [2048, 1024], P(('rep', 'cp'), 'tp'), parts along dimension 0, may hold values from -6 to 6
- segment_ids: int32 [2048], P(('rep', 'cp')), parts along dimension 0, may hold values from 0 to 3, never falling along the last dimension, each value on 1 to 768 neighbouring positions
Outputs:
- attended: bfloat16 [2048, 8192], P(('rep', 'cp'), 'tp'), parts along dimension 0
The draws below stay inside these ranges and needn't reach their ends.
There are 2 independent parts, one for each index of `rep`. The reference program is written for one: setup_inputs(seed, part) draws one part's arguments, and reference() takes and returns one part's arrays. A program takes and returns all parts, laid end to end along the dimension named above; each array names one. Nothing has to cross between parts.
Inputs may be any that keep to these rules, and one draw needn't show every extreme that they name: `segment_ids`: segment ids never fall along the sequence of one part.
All inputs are finite; a program needn't handle non-finite values.
Results may differ from the reference program's by a relative error of at most 0.012.
Values may be sent and summed in bfloat16 or wider, within the bound.
A program may use at most 64 MiB of HBM per device.

```python
import math
import jax
import jax.numpy as jnp
import numpy as np
from jax import lax

HEADS = 64
KV_HEADS = 8
HEAD_DIM = 128
TOK_DEV = 256
LENGTH = 1024
N_CP = 4


def drawn_pair(key):
    base = jax.random.fold_in(key, 31)
    key_q, key_k = jax.random.split(base, 2)
    query_all = jnp.clip(jax.random.normal(key_q, (LENGTH, HEADS, HEAD_DIM), jnp.float32), -4.0, 4.0)
    key_all = jnp.clip(jax.random.normal(key_k, (LENGTH, KV_HEADS, HEAD_DIM), jnp.float32), -4.0, 4.0)
    return (query_all.reshape(LENGTH, HEADS * HEAD_DIM), key_all.reshape(LENGTH, KV_HEADS * HEAD_DIM))


def draw_queries(key, part):
    return drawn_pair(key)[0].astype(jnp.bfloat16)


def draw_keys(key, part):
    return drawn_pair(key)[1].astype(jnp.bfloat16)


def steps_of(rng, extent, pieces, low, largest):
    loudness = 1.0
    for position, shards_of in pieces:
        heights = jax.random.uniform(jax.random.fold_in(jax.random.fold_in(rng, 6), position), (shards_of,), jnp.float32, low / len(pieces), largest / len(pieces))
        loudness = loudness * jnp.repeat(jnp.exp(heights), extent[position] // shards_of).reshape((-1,) + (1,) * (len(extent) - 1 - position))
    return loudness


def split_up(number_of, total, most, skew):
    weights = [(1 << 20) // math.isqrt(rank ** skew) + 1 for rank in range(2, number_of + 1)]
    spare, given = total - most - (number_of - 1), [1] * (number_of - 1)
    while spare > 0:
        free = [i for i in range(number_of - 1) if given[i] < most]
        whole, left = sum([weights[i] for i in free]), spare
        for i in free:
            addition = min(most - given[i], max(1, left * weights[i] // whole), spare)
            given[i] = given[i] + addition
            spare = spare - addition
    return np.array([most] + given)


def uneven(key, number_of, total, reach, skew):
    if number_of == 2:
        one = jax.random.randint(key, (), max(1, total - reach), min(reach, total - 1) + 1)
        return jnp.stack([one, total - one])
    tallies = jnp.asarray(split_up(number_of, total, reach, skew), jnp.int32)
    pairs = (number_of - 1) // 2
    source_of, sink = tallies[1:1 + 2 * pairs:2], tallies[2:2 + 2 * pairs:2]
    slack = jnp.minimum(source_of - 1, reach - sink)
    moved = jax.random.randint(jax.random.fold_in(key, 1), (pairs,), 0, 1 << 20) % (slack + 1)
    tallies = tallies.at[1:1 + 2 * pairs:2].set(source_of - moved).at[2:2 + 2 * pairs:2].set(sink + moved)
    return tallies[jax.random.permutation(jax.random.fold_in(key, 2), number_of)]


def centred(key, shape, spread, most, cuts=(), kind=jnp.bfloat16):
    values = jax.random.normal(key, shape, jnp.float32) * spread
    if len(cuts) > 0:
        values = steps_of(key, shape, cuts, -0.22, 0.18) * values
    return jnp.clip(values, min=-most, max=most).astype(kind)


def setup_inputs(seed: int = 0, part: int = 0) -> dict:
    splits = jax.random.split(jax.random.key(seed), 5)
    part_keys = jax.random.split(jax.random.fold_in(splits[4], part), 5)
    queries = draw_queries(jax.random.fold_in(jax.random.fold_in(splits[4], part), 71), part)
    keys = draw_keys(jax.random.fold_in(jax.random.fold_in(splits[4], part), 71), part)
    values = centred(part_keys[2], (LENGTH, KV_HEADS * HEAD_DIM), 1.0, 6.0, ((0, 4), (1, 4)))
    segment_ids = jnp.searchsorted(jnp.cumsum(uneven(part_keys[3], N_CP, LENGTH, TOK_DEV * N_CP * 3 // 4, 2)), jnp.arange(LENGTH), side="right").astype(jnp.int32)
    return dict(queries=queries, keys=keys, values=values, segment_ids=segment_ids)


rope_base = 500000.0

def rotate(vectors, positions):
    half = vectors.shape[-1] // 2
    freq = rope_base ** (-jnp.arange(half, dtype=jnp.float32) * 2.0 / vectors.shape[-1])
    angle = positions.astype(jnp.float32)[:, None] * freq[None, :]
    cosine = jnp.cos(angle)[:, None, :]
    sine = jnp.sin(angle)[:, None, :]
    first = vectors[..., :half]
    second = vectors[..., half:]
    return jnp.concatenate([first * cosine - second * sine, second * cosine + first * sine], axis=-1)

def reference(queries, keys, values, segment_ids):
    total_len = queries.shape[0]
    index = jnp.arange(total_len, dtype=jnp.int32)
    starts = jnp.searchsorted(segment_ids, segment_ids, side='left').astype(jnp.int32)
    positions = index - starts
    group = HEADS // KV_HEADS
    rot_q = rotate(queries.astype(jnp.float32).reshape(total_len, HEADS, HEAD_DIM), positions).astype(jnp.bfloat16)
    rot_k = rotate(keys.astype(jnp.float32).reshape(total_len, KV_HEADS, HEAD_DIM), positions).astype(jnp.bfloat16)
    key_heads = jnp.moveaxis(rot_k, 1, 0).astype(jnp.float32)
    value_heads = jnp.moveaxis(values.reshape(total_len, KV_HEADS, HEAD_DIM), 1, 0).astype(jnp.float32)
    block = math.gcd(total_len, 512)
    count = total_len // block
    query_blocks = rot_q.reshape(count, block, KV_HEADS, group, HEAD_DIM)
    scale = 1.0 / math.sqrt(HEAD_DIM)

    def one_block(packed):
        query_block, number = packed
        row_index = number * block + jnp.arange(block, dtype=jnp.int32)
        row_start = lax.dynamic_slice_in_dim(starts, (number * block).astype(jnp.int32), block)
        keep = (index[None, :] <= row_index[:, None]) & (index[None, :] >= row_start[:, None])
        per_head = jnp.moveaxis(query_block, 1, 0).astype(jnp.float32)

        def one_head(triple):
            query_head, key_head, value_head = triple
            scores = jnp.einsum('tjd,kd->jtk', query_head, key_head) * scale
            scores = jnp.where(keep[None], scores, -1e+30)
            top = lax.optimization_barrier(jnp.max(scores, axis=-1, keepdims=True))
            weights = jnp.where(keep[None], jnp.exp(scores - top), 0.0)
            totals = lax.optimization_barrier(jnp.sum(weights, axis=-1))
            weights_low = weights.astype(jnp.bfloat16).astype(jnp.float32)
            summed = jnp.einsum('jtk,kd->tjd', weights_low, value_head)
            return summed / jnp.transpose(totals)[:, :, None]
        outputs = lax.map(one_head, (per_head, key_heads, value_heads))
        return jnp.moveaxis(outputs, 0, 1)
    results = lax.map(one_block, (query_blocks, jnp.arange(count, dtype=jnp.int32)))
    return results.reshape(total_len, HEADS * HEAD_DIM).astype(jnp.bfloat16)
```

```python
import functools
import math

import jax
import jax.numpy as jnp
import numpy as np
from jax import lax
from jax.experimental import pallas as pl
from jax.experimental.pallas import tpu as pltpu
from jax.sharding import PartitionSpec as P

HEAD_DIM = 128
ROPE_BASE = 500000.0
HIDDEN = -1e30
MESH = pl.DeviceIdType.MESH


def tables(rows, blocks):
    half = HEAD_DIM // 2
    freq = ROPE_BASE ** (-np.arange(half, dtype=np.float64) * 2.0 / HEAD_DIM)
    sign = np.concatenate([-np.ones(half), np.ones(half)])

    def pair(positions):
        angle = np.tile(positions[:, None] * freq[None, :], (1, 2))
        return np.cos(angle), np.sin(angle) * sign

    local = np.stack(pair(np.arange(rows, dtype=np.float64)))
    base = np.stack(pair(np.arange(blocks, dtype=np.float64) * rows), axis=1)
    return local.astype(np.float32), base.astype(np.float32)


def attend(
    n, chunks, q_hbm, k_hbm, v_hbm, id_hbm, local_hbm, base_ref, out_ref,
    q_raw, q_turned, k_buf, v_buf, id_buf, local, bias, acc, top, total,
    q_sem, own_sem, send_sem, recv_sem,
):
    me = lax.axis_index("cp")
    rows = q_hbm.shape[0]
    heads = q_hbm.shape[1] // HEAD_DIM
    kv_heads = k_hbm.shape[1] // HEAD_DIM
    group = heads // kv_heads
    chunk = rows // chunks
    right = jnp.minimum(me + 1, n - 1)
    left = jnp.maximum(me - 1, 0)

    barrier = pltpu.get_barrier_semaphore()

    @pl.when(me > 0)
    def _():
        pl.semaphore_signal(barrier, inc=1, device_id={"cp": left}, device_id_type=MESH)

    def pieces(slot):
        out = [(None, id_buf.at[slot])]
        for c in range(chunks):
            part = pl.ds(c * chunk, chunk)
            out.append((k_hbm.at[part, :], k_buf.at[slot, part, :]))
            out.append((v_hbm.at[part, :], v_buf.at[slot, part, :]))
        return out

    def of_chunk(c):
        return ([0] if c == 0 else []) + [1 + 2 * c, 2 + 2 * c]

    def own_copies():
        source = [id_hbm] + [s for s, _ in pieces(0)[1:]]
        return [
            pltpu.make_async_copy(source[p], pieces(0)[p][1], own_sem.at[p])
            for p in range(1 + 2 * chunks)
        ]

    def remote(p, slot, source):
        return pltpu.make_async_remote_copy(
            src_ref=source,
            dst_ref=pieces(slot)[p][1],
            send_sem=send_sem.at[slot - 1, p],
            recv_sem=recv_sem.at[slot - 1, p],
            device_id={"cp": right},
            device_id_type=MESH,
        )

    def own_remote(p):
        return remote(p, 1, id_hbm if p == 0 else pieces(0)[p][0])

    q_copies = [pltpu.make_async_copy(q_hbm, q_raw, q_sem.at[0]),
                pltpu.make_async_copy(local_hbm, local, q_sem.at[1])]
    for copy in own_copies() + q_copies:
        copy.start()

    @pl.when(me < n - 1)
    def _():
        pl.semaphore_wait(barrier, 1)
        for p in range(1 + 2 * chunks):
            own_remote(p).start()

    def phases(block, start, size):
        row = base_ref[block]
        cb, sb = row[0:1, :], row[1:2, :]
        cr = local[0, pl.ds(start, size), :]
        sr = local[1, pl.ds(start, size), :]
        return cb * cr - sb * sr, sb * cr + cb * sr

    def turn(x, cosine, sine):
        x = x.astype(jnp.float32)
        return x * cosine + pltpu.roll(x, HEAD_DIM // 2, axis=1) * sine

    for copy in q_copies:
        copy.wait()
    cosine, sine = phases(me, 0, rows)
    scale = math.log2(math.e) / math.sqrt(HEAD_DIM)
    cosine, sine = cosine * scale, sine * scale
    for h in range(heads):
        x = turn(q_raw[:, h * HEAD_DIM:(h + 1) * HEAD_DIM], cosine, sine)
        q_turned[h] = x.T.astype(jnp.bfloat16)
    acc[...] = jnp.zeros_like(acc)
    total[...] = jnp.zeros_like(total)
    top[...] = jnp.full_like(top, HIDDEN)
    for copy in own_copies():
        copy.wait()

    row_index = lax.broadcasted_iota(jnp.int32, (chunk, rows), 1)
    key_index = lax.broadcasted_iota(jnp.int32, (chunk, rows), 0)

    def step(k, unused):
        block = me - k
        for c in range(chunks):
            @pl.when(k > 0)
            def _():
                for p in of_chunk(c):
                    remote(p, k, pieces(k)[p][1]).wait_recv()

            @pl.when((k > 0) & (me < n - 1))
            def _():
                for p in of_chunk(c):
                    remote(p, k + 1, pieces(k)[p][1]).start()

            part = pl.ds(c * chunk, chunk)
            row_id = id_buf[0].astype(jnp.float32)
            key_id = id_buf[k, :, part].astype(jnp.float32)
            key_id = jnp.broadcast_to(key_id, (HEAD_DIM, chunk)).T[:, :1]
            keep = (key_id == row_id) & (key_index + (c * chunk - k * rows) <= row_index)
            bias[...] = jnp.where(keep, 0.0, HIDDEN)
            cosine, sine = phases(block, c * chunk, chunk)
            for g in range(kv_heads):
                lanes = slice(g * HEAD_DIM, (g + 1) * HEAD_DIM)
                key = turn(k_buf[k, part, lanes], cosine, sine).astype(jnp.bfloat16)
                value = v_buf[k, part, lanes].T
                for h in range(g * group, (g + 1) * group):
                    scores = jnp.dot(key, q_turned[h], preferred_element_type=jnp.float32)
                    scores = scores + bias[...]
                    old = top[h:h + 1, :]
                    new = jnp.maximum(old, jnp.max(scores, axis=0, keepdims=True))
                    weights = jnp.exp2(scores - new)
                    factor = jnp.exp2(old - new)
                    top[h:h + 1, :] = new
                    total[h:h + 1, :] = total[h:h + 1, :] * factor + jnp.sum(
                        weights, axis=0, keepdims=True
                    )
                    acc[h] = acc[h] * factor + jnp.dot(
                        value, weights.astype(jnp.bfloat16), preferred_element_type=jnp.float32
                    )
        return unused

    lax.fori_loop(0, me + 1, step, 0)

    for h in range(heads):
        result = acc[h] * (1.0 / total[h:h + 1, :])
        out_ref[:, h * HEAD_DIM:(h + 1) * HEAD_DIM] = result.T.astype(out_ref.dtype)

    @pl.when(me < n - 1)
    def _():
        for p in range(1 + 2 * chunks):
            own_remote(p).wait_send()

        def drain(k, unused):
            for p in range(1 + 2 * chunks):
                remote(p, k + 1, pieces(k)[p][1]).wait_send()
            return unused

        lax.fori_loop(1, me + 1, drain, 0)


def body(n, queries, keys, values, segment_ids):
    rows, width = queries.shape
    kv_width = keys.shape[1]
    heads = width // HEAD_DIM
    chunks = 2
    chunk = rows // chunks
    local, base = tables(rows, n)
    anywhere = pl.BlockSpec(memory_space=pl.ANY)
    vmem = pl.BlockSpec(memory_space=pltpu.VMEM)
    count = 1 + 2 * chunks
    return pl.pallas_call(
        functools.partial(attend, n, chunks),
        out_shape=jax.ShapeDtypeStruct((rows, width), queries.dtype),
        in_specs=[anywhere] * 5 + [vmem],
        out_specs=vmem,
        scratch_shapes=[
            pltpu.VMEM((rows, width), queries.dtype),
            pltpu.VMEM((heads, HEAD_DIM, rows), jnp.bfloat16),
            pltpu.VMEM((n, rows, kv_width), keys.dtype),
            pltpu.VMEM((n, rows, kv_width), values.dtype),
            pltpu.VMEM((n, 1, rows), jnp.int32),
            pltpu.VMEM((2, rows, HEAD_DIM), jnp.float32),
            pltpu.VMEM((chunk, rows), jnp.float32),
            pltpu.VMEM((heads, HEAD_DIM, rows), jnp.float32),
            pltpu.VMEM((heads, rows), jnp.float32),
            pltpu.VMEM((heads, rows), jnp.float32),
            pltpu.SemaphoreType.DMA((2,)),
            pltpu.SemaphoreType.DMA((count,)),
            pltpu.SemaphoreType.DMA((max(n - 1, 1), count)),
            pltpu.SemaphoreType.DMA((max(n - 1, 1), count)),
        ],
        compiler_params=pltpu.CompilerParams(collective_id=0, has_side_effects=True),
    )(queries, keys, values, segment_ids.reshape(1, rows), jnp.asarray(local), jnp.asarray(base))


def solution(mesh):
    return jax.shard_map(
        functools.partial(body, mesh.shape["cp"]),
        mesh=mesh,
        in_specs=(
            P(("rep", "cp"), "tp"),
            P(("rep", "cp"), "tp"),
            P(("rep", "cp"), "tp"),
            P(("rep", "cp")),
        ),
        out_specs=P(("rep", "cp"), "tp"),
        check_vma=False,
    )
```

```python
import functools
import math

import jax
import jax.numpy as jnp
import numpy as np
from jax import lax
from jax.experimental import pallas as pl
from jax.experimental.pallas import tpu as pltpu
from jax.sharding import PartitionSpec as P

HEAD_DIM = 128
ROPE_BASE = 500000.0
HIDDEN = -1e30
MESH = pl.DeviceIdType.MESH


def tables(rows, blocks):
    half = HEAD_DIM // 2
    freq = ROPE_BASE ** (-np.arange(half, dtype=np.float64) * 2.0 / HEAD_DIM)
    sign = np.concatenate([-np.ones(half), np.ones(half)])

    def pair(positions):
        angle = np.tile(positions[:, None] * freq[None, :], (1, 2))
        return np.cos(angle), np.sin(angle) * sign

    local = np.stack(pair(np.arange(rows, dtype=np.float64)))
    base = np.stack(pair(np.arange(blocks, dtype=np.float64) * rows), axis=1)
    return local.astype(np.float32), base.astype(np.float32)


def attend(
    n, chunks, q_hbm, k_hbm, v_hbm, id_hbm, local_hbm, base_hbm, out_ref,
    q_raw, q_turned, k_buf, v_buf, id_buf, local, base_ref, id_column, bias, acc, top, total,
    q_sem, own_sem, send_sem, recv_sem,
):
    me = lax.axis_index("cp")
    rows = q_hbm.shape[0]
    heads = q_hbm.shape[1] // HEAD_DIM
    kv_heads = k_hbm.shape[1] // HEAD_DIM
    group = heads // kv_heads
    chunk = rows // chunks
    right = jnp.minimum(me + 1, n - 1)
    left = jnp.maximum(me - 1, 0)

    barrier = pltpu.get_barrier_semaphore()

    @pl.when(me > 0)
    def _():
        pl.semaphore_signal(barrier, inc=1, device_id={"cp": left}, device_id_type=MESH)

    def span(c):
        return pl.ds(pl.multiple_of(c * chunk, chunk), chunk)

    def key_part(slot, c):
        return k_buf.at[slot, span(c), :]

    def value_part(slot, c):
        return v_buf.at[slot, span(c), :]

    own_copies = [
        pltpu.make_async_copy(id_hbm, id_buf.at[0], own_sem.at[0]),
        pltpu.make_async_copy(k_hbm, k_buf.at[0], own_sem.at[1]),
        pltpu.make_async_copy(v_hbm, v_buf.at[0], own_sem.at[2]),
    ]

    def remote(piece, source, target, slot):
        return pltpu.make_async_remote_copy(
            src_ref=source,
            dst_ref=target,
            send_sem=send_sem.at[slot, piece],
            recv_sem=recv_sem.at[slot, piece],
            device_id={"cp": right},
            device_id_type=MESH,
        )

    def id_hop(slot):
        return remote(0, id_buf.at[slot], id_buf.at[slot + 1], slot)

    def key_hop(slot, c):
        return remote(1 + 2 * c, key_part(slot, c), key_part(slot + 1, c), slot)

    def value_hop(slot, c):
        return remote(2 + 2 * c, value_part(slot, c), value_part(slot + 1, c), slot)

    def send(slot, c):
        @pl.when(c == 0)
        def _():
            id_hop(slot).start()

        key_hop(slot, c).start()
        value_hop(slot, c).start()

    q_copies = [pltpu.make_async_copy(q_hbm, q_raw, q_sem.at[0]),
                pltpu.make_async_copy(local_hbm, local, q_sem.at[1]),
                pltpu.make_async_copy(base_hbm, base_ref, q_sem.at[2])]
    for copy in own_copies + q_copies:
        copy.start()
    for copy in own_copies:
        copy.wait()

    @pl.when(me < n - 1)
    def _():
        pl.semaphore_wait(barrier, 1)
        for c in range(chunks):
            send(0, c)

    def phases(block, start, size):
        row = base_ref[block]
        cb, sb = row[0:1, :], row[1:2, :]
        cr = local[0, pl.ds(start, size), :]
        sr = local[1, pl.ds(start, size), :]
        return cb * cr - sb * sr, sb * cr + cb * sr

    def turn(x, cosine, sine):
        x = x.astype(jnp.float32)
        return x * cosine + pltpu.roll(x, HEAD_DIM // 2, axis=1) * sine

    for copy in q_copies:
        copy.wait()
    cosine, sine = phases(me, 0, rows)
    scale = math.log2(math.e) / math.sqrt(HEAD_DIM)
    cosine, sine = cosine * scale, sine * scale
    for h in range(heads):
        x = turn(q_raw[:, h * HEAD_DIM:(h + 1) * HEAD_DIM], cosine, sine)
        q_turned[h] = x.T.astype(jnp.bfloat16)
    acc[...] = jnp.zeros_like(acc)
    total[...] = jnp.zeros_like(total)
    top[...] = jnp.full_like(top, HIDDEN)
    row_index = lax.broadcasted_iota(jnp.int32, (chunk, rows), 1)
    key_index = lax.broadcasted_iota(jnp.int32, (chunk, rows), 0)

    def step(t, unused):
        k, c = t // chunks, t % chunks

        @pl.when(k > 0)
        def _():
            @pl.when(c == 0)
            def _():
                id_hop(k - 1).wait_recv()

            key_hop(k - 1, c).wait_recv()
            value_hop(k - 1, c).wait_recv()

            @pl.when(me < n - 1)
            def _():
                send(k, c)

        @pl.when(c == 0)
        def _():
            key_id = id_buf[k].astype(jnp.float32)
            id_column[...] = jnp.broadcast_to(key_id, (HEAD_DIM, rows)).T

        row_id = id_buf[0].astype(jnp.float32)
        key_id = id_column[span(c), :][:, :1]
        keep = (key_id == row_id) & (key_index + (c * chunk - k * rows) <= row_index)
        bias[...] = jnp.where(keep, 0.0, HIDDEN)
        cosine, sine = phases(me - k, pl.multiple_of(c * chunk, chunk), chunk)
        for g in range(kv_heads):
            lanes = slice(g * HEAD_DIM, (g + 1) * HEAD_DIM)
            key = turn(k_buf[k, span(c), lanes], cosine, sine).astype(jnp.bfloat16)
            value = v_buf[k, span(c), lanes].T
            for h in range(g * group, (g + 1) * group):
                scores = jnp.dot(key, q_turned[h], preferred_element_type=jnp.float32)
                scores = scores + bias[...]
                old = top[h:h + 1, :]
                new = jnp.maximum(old, jnp.max(scores, axis=0, keepdims=True))
                weights = jnp.exp2(scores - new)
                factor = jnp.exp2(old - new)
                top[h:h + 1, :] = new
                total[h:h + 1, :] = total[h:h + 1, :] * factor + jnp.sum(
                    weights, axis=0, keepdims=True
                )
                acc[h] = acc[h] * factor + jnp.dot(
                    value, weights.astype(jnp.bfloat16), preferred_element_type=jnp.float32
                )
        return unused

    lax.fori_loop(0, (me + 1) * chunks, step, 0)

    for h in range(heads):
        result = acc[h] * (1.0 / total[h:h + 1, :])
        out_ref[:, h * HEAD_DIM:(h + 1) * HEAD_DIM] = result.T.astype(out_ref.dtype)

    @pl.when(me < n - 1)
    def _():
        def drain(k, unused):
            id_hop(k).wait_send()
            for c in range(chunks):
                key_hop(k, c).wait_send()
                value_hop(k, c).wait_send()
            return unused

        lax.fori_loop(0, me + 1, drain, 0)


def body(n, queries, keys, values, segment_ids):
    rows, width = queries.shape
    kv_width = keys.shape[1]
    heads = width // HEAD_DIM
    chunks = 2
    chunk = rows // chunks
    local, base = tables(rows, n)
    anywhere = pl.BlockSpec(memory_space=pl.ANY)
    vmem = pl.BlockSpec(memory_space=pltpu.VMEM)
    count = 1 + 2 * chunks
    return pl.pallas_call(
        functools.partial(attend, n, chunks),
        out_shape=pltpu.VMEM((rows, width), queries.dtype),
        in_specs=[anywhere] * 6,
        out_specs=vmem,
        scratch_shapes=[
            pltpu.VMEM((rows, width), queries.dtype),
            pltpu.VMEM((heads, HEAD_DIM, rows), jnp.bfloat16),
            pltpu.VMEM((n, rows, kv_width), keys.dtype),
            pltpu.VMEM((n, rows, kv_width), values.dtype),
            pltpu.VMEM((n, 1, rows), jnp.int32),
            pltpu.VMEM((2, rows, HEAD_DIM), jnp.float32),
            pltpu.VMEM((n, 2, HEAD_DIM), jnp.float32),
            pltpu.VMEM((rows, HEAD_DIM), jnp.float32),
            pltpu.VMEM((chunk, rows), jnp.float32),
            pltpu.VMEM((heads, HEAD_DIM, rows), jnp.float32),
            pltpu.VMEM((heads, rows), jnp.float32),
            pltpu.VMEM((heads, rows), jnp.float32),
            pltpu.SemaphoreType.DMA((3,)),
            pltpu.SemaphoreType.DMA((3,)),
            pltpu.SemaphoreType.DMA((max(n - 1, 1), count)),
            pltpu.SemaphoreType.DMA((max(n - 1, 1), count)),
        ],
        compiler_params=pltpu.CompilerParams(collective_id=0, has_side_effects=True),
    )(queries, keys, values, segment_ids.reshape(1, rows), jnp.asarray(local), jnp.asarray(base))


def solution(mesh):
    return jax.shard_map(
        functools.partial(body, mesh.shape["cp"]),
        mesh=mesh,
        in_specs=(
            P(("rep", "cp"), "tp"),
            P(("rep", "cp"), "tp"),
            P(("rep", "cp"), "tp"),
            P(("rep", "cp")),
        ),
        out_specs=P(("rep", "cp"), "tp"),
        check_vma=False,
    )
```

```python
import functools
import math

import jax
import jax.numpy as jnp
import numpy as np
from jax import lax
from jax.experimental import pallas as pl
from jax.experimental.pallas import tpu as pltpu
from jax.sharding import PartitionSpec as P

HEAD_DIM = 128
ROPE_BASE = 500000.0
HIDDEN = -1e30
MESH = pl.DeviceIdType.MESH


def tables(rows, blocks):
    half = HEAD_DIM // 2
    freq = ROPE_BASE ** (-np.arange(half, dtype=np.float64) * 2.0 / HEAD_DIM)
    sign = np.concatenate([-np.ones(half), np.ones(half)])

    def pair(positions):
        angle = np.tile(positions[:, None] * freq[None, :], (1, 2))
        return np.cos(angle), np.sin(angle) * sign

    local = np.stack(pair(np.arange(rows, dtype=np.float64)))
    base = np.stack(pair(np.arange(blocks, dtype=np.float64) * rows), axis=1)
    return local.astype(np.float32), base.astype(np.float32)


def attend(
    n, chunks, q_hbm, k_hbm, v_hbm, id_hbm, local_hbm, base_hbm, out_ref,
    q_raw, q_turned, k_buf, v_buf, id_buf, local, base_ref, id_column, bias, weights, factor, acc, top, total,
    q_sem, own_sem, send_sem, recv_sem,
):
    me = lax.axis_index("cp")
    rows = q_hbm.shape[0]
    heads = q_hbm.shape[1] // HEAD_DIM
    kv_heads = k_hbm.shape[1] // HEAD_DIM
    group = heads // kv_heads
    chunk = rows // chunks
    right = jnp.minimum(me + 1, n - 1)
    left = jnp.maximum(me - 1, 0)

    barrier = pltpu.get_barrier_semaphore()

    @pl.when(me > 0)
    def _():
        pl.semaphore_signal(barrier, inc=1, device_id={"cp": left}, device_id_type=MESH)

    def span(c):
        return pl.ds(pl.multiple_of(c * chunk, chunk), chunk)

    def key_part(slot, c):
        return k_buf.at[slot, span(c), :]

    def value_part(slot, c):
        return v_buf.at[slot, span(c), :]

    own_copies = [
        pltpu.make_async_copy(id_hbm, id_buf.at[0], own_sem.at[0]),
        pltpu.make_async_copy(k_hbm, k_buf.at[0], own_sem.at[1]),
        pltpu.make_async_copy(v_hbm, v_buf.at[0], own_sem.at[2]),
    ]

    def remote(piece, source, target, slot):
        return pltpu.make_async_remote_copy(
            src_ref=source,
            dst_ref=target,
            send_sem=send_sem.at[slot, piece],
            recv_sem=recv_sem.at[slot, piece],
            device_id={"cp": right},
            device_id_type=MESH,
        )

    def id_hop(slot):
        return remote(0, id_buf.at[slot], id_buf.at[slot + 1], slot)

    def key_hop(slot, c):
        return remote(1 + 2 * c, key_part(slot, c), key_part(slot + 1, c), slot)

    def value_hop(slot, c):
        return remote(2 + 2 * c, value_part(slot, c), value_part(slot + 1, c), slot)

    q_copies = [pltpu.make_async_copy(q_hbm, q_raw, q_sem.at[0]),
                pltpu.make_async_copy(local_hbm, local, q_sem.at[1]),
                pltpu.make_async_copy(base_hbm, base_ref, q_sem.at[2])]
    for copy in own_copies + q_copies:
        copy.start()
    for copy in own_copies:
        copy.wait()

    @pl.when(me < n - 1)
    def _():
        pl.semaphore_wait(barrier, 1)
        id_hop(0).start()
        for c in range(chunks):
            key_hop(0, c).start()
        for c in range(chunks):
            value_hop(0, c).start()

    def phases(block, start, size):
        row = base_ref[block]
        cb, sb = row[0:1, :], row[1:2, :]
        cr = local[0, pl.ds(start, size), :]
        sr = local[1, pl.ds(start, size), :]
        return cb * cr - sb * sr, sb * cr + cb * sr

    def turn(x, cosine, sine):
        x = x.astype(jnp.float32)
        return x * cosine + pltpu.roll(x, HEAD_DIM // 2, axis=1) * sine

    for copy in q_copies:
        copy.wait()
    cosine, sine = phases(me, 0, rows)
    scale = math.log2(math.e) / math.sqrt(HEAD_DIM)
    cosine, sine = cosine * scale, sine * scale
    for h in range(heads):
        x = turn(q_raw[:, h * HEAD_DIM:(h + 1) * HEAD_DIM], cosine, sine)
        q_turned[h] = x.T.astype(jnp.bfloat16)
    acc[...] = jnp.zeros_like(acc)
    total[...] = jnp.zeros_like(total)
    top[...] = jnp.full_like(top, HIDDEN)
    row_index = lax.broadcasted_iota(jnp.int32, (chunk, rows), 1)
    key_index = lax.broadcasted_iota(jnp.int32, (chunk, rows), 0)

    def weigh(k, c):
        @pl.when(k > 0)
        def _():
            @pl.when(c == 0)
            def _():
                id_hop(k - 1).wait_recv()

            key_hop(k - 1, c).wait_recv()

            @pl.when(me < n - 1)
            def _():
                @pl.when(c == 0)
                def _():
                    id_hop(k).start()

                key_hop(k, c).start()

        @pl.when(c == 0)
        def _():
            key_id = id_buf[k].astype(jnp.float32)
            id_column[...] = jnp.broadcast_to(key_id, (HEAD_DIM, rows)).T

        row_id = id_buf[0].astype(jnp.float32)
        key_id = id_column[span(c), :][:, :1]
        keep = (key_id == row_id) & (key_index + (c * chunk - k * rows) <= row_index)
        bias[...] = jnp.where(keep, 0.0, HIDDEN)
        cosine, sine = phases(me - k, pl.multiple_of(c * chunk, chunk), chunk)
        for g in range(kv_heads):
            lanes = slice(g * HEAD_DIM, (g + 1) * HEAD_DIM)
            key = turn(k_buf[k, span(c), lanes], cosine, sine).astype(jnp.bfloat16)
            for h in range(g * group, (g + 1) * group):
                scores = jnp.dot(key, q_turned[h], preferred_element_type=jnp.float32)
                scores = scores + bias[...]
                old = top[h:h + 1, :]
                new = jnp.maximum(old, jnp.max(scores, axis=0, keepdims=True))
                weight = jnp.exp2(scores - new)
                change = jnp.exp2(old - new)
                top[h:h + 1, :] = new
                factor[c, h:h + 1, :] = change
                total[h:h + 1, :] = total[h:h + 1, :] * change + jnp.sum(
                    weight, axis=0, keepdims=True
                )
                weights[c, h] = weight.astype(jnp.bfloat16)

    def gather(k, c, store):
        @pl.when(k > 0)
        def _():
            value_hop(k - 1, c).wait_recv()

            @pl.when(me < n - 1)
            def _():
                value_hop(k, c).start()

        for g in range(kv_heads):
            lanes = slice(g * HEAD_DIM, (g + 1) * HEAD_DIM)
            value = v_buf[k, span(c), lanes].T
            for h in range(g * group, (g + 1) * group):
                store(h, acc[h] * factor[c, h:h + 1, :] + jnp.dot(
                    value, weights[c, h], preferred_element_type=jnp.float32
                ))

    def keep_sum(h, result):
        acc[h] = result

    def finish(h, result):
        result = result * (1.0 / total[h:h + 1, :])
        out_ref[:, h * HEAD_DIM:(h + 1) * HEAD_DIM] = result.T.astype(out_ref.dtype)

    def step(t, unused):
        k, c = t // (2 * chunks), t % (2 * chunks)

        @pl.when(c < chunks)
        def _():
            weigh(k, c)

        @pl.when(c >= chunks)
        def _():
            gather(k, c - chunks, keep_sum)

        return unused

    lax.fori_loop(0, (me + 1) * 2 * chunks - 1, step, 0)
    gather(me, chunks - 1, finish)

    @pl.when(me < n - 1)
    def _():
        def drain(k, unused):
            id_hop(k).wait_send()
            for c in range(chunks):
                key_hop(k, c).wait_send()
                value_hop(k, c).wait_send()
            return unused

        lax.fori_loop(0, me + 1, drain, 0)


def body(n, queries, keys, values, segment_ids):
    rows, width = queries.shape
    kv_width = keys.shape[1]
    heads = width // HEAD_DIM
    chunks = 2
    chunk = rows // chunks
    local, base = tables(rows, n)
    anywhere = pl.BlockSpec(memory_space=pl.ANY)
    vmem = pl.BlockSpec(memory_space=pltpu.VMEM)
    count = 1 + 2 * chunks
    return pl.pallas_call(
        functools.partial(attend, n, chunks),
        out_shape=pltpu.VMEM((rows, width), queries.dtype),
        in_specs=[anywhere] * 6,
        out_specs=vmem,
        scratch_shapes=[
            pltpu.VMEM((rows, width), queries.dtype),
            pltpu.VMEM((heads, HEAD_DIM, rows), jnp.bfloat16),
            pltpu.VMEM((n, rows, kv_width), keys.dtype),
            pltpu.VMEM((n, rows, kv_width), values.dtype),
            pltpu.VMEM((n, 1, rows), jnp.int32),
            pltpu.VMEM((2, rows, HEAD_DIM), jnp.float32),
            pltpu.VMEM((n, 2, HEAD_DIM), jnp.float32),
            pltpu.VMEM((rows, HEAD_DIM), jnp.float32),
            pltpu.VMEM((chunk, rows), jnp.float32),
            pltpu.VMEM((chunks, heads, chunk, rows), jnp.bfloat16),
            pltpu.VMEM((chunks, heads, rows), jnp.float32),
            pltpu.VMEM((heads, HEAD_DIM, rows), jnp.float32),
            pltpu.VMEM((heads, rows), jnp.float32),
            pltpu.VMEM((heads, rows), jnp.float32),
            pltpu.SemaphoreType.DMA((3,)),
            pltpu.SemaphoreType.DMA((3,)),
            pltpu.SemaphoreType.DMA((max(n - 1, 1), count)),
            pltpu.SemaphoreType.DMA((max(n - 1, 1), count)),
        ],
        compiler_params=pltpu.CompilerParams(collective_id=0, has_side_effects=True),
    )(queries, keys, values, segment_ids.reshape(1, rows), jnp.asarray(local), jnp.asarray(base))


def solution(mesh):
    return jax.shard_map(
        functools.partial(body, mesh.shape["cp"]),
        mesh=mesh,
        in_specs=(
            P(("rep", "cp"), "tp"),
            P(("rep", "cp"), "tp"),
            P(("rep", "cp"), "tp"),
            P(("rep", "cp")),
        ),
        out_specs=P(("rep", "cp"), "tp"),
        check_vma=False,
    )
```

```python
import functools
import math

import jax
import jax.numpy as jnp
import numpy as np
from jax import lax
from jax.experimental import pallas as pl
from jax.experimental.pallas import tpu as pltpu
from jax.sharding import PartitionSpec as P

HEAD_DIM = 128
ROPE_BASE = 500000.0
HIDDEN = -1e30
BURST = 4
VMEM_LIMIT = 32 << 20
MESH = pl.DeviceIdType.MESH


def tables(rows, blocks):
    half = HEAD_DIM // 2
    freq = ROPE_BASE ** (-np.arange(half, dtype=np.float64) * 2.0 / HEAD_DIM)
    sign = np.concatenate([-np.ones(half), np.ones(half)])

    def pair(positions):
        angle = np.tile(positions[:, None] * freq[None, :], (1, 2))
        return np.cos(angle), np.sin(angle) * sign

    local = np.stack(pair(np.arange(rows, dtype=np.float64)))
    base = np.stack(pair(np.arange(blocks, dtype=np.float64) * rows), axis=1)
    return local.astype(np.float32), base.astype(np.float32)


def attend(
    n, chunks, q_hbm, k_hbm, v_hbm, id_hbm, local_hbm, base_hbm,
    acc, weights, factor, total, v_last,
    q_raw, q_turned, k_buf, v_buf, id_buf, local, base_ref, id_column, bias, top,
    q_sem, own_sem, send_sem, recv_sem,
):
    me = lax.axis_index("cp")
    rows = q_hbm.shape[0]
    heads = q_hbm.shape[1] // HEAD_DIM
    kv_heads = k_hbm.shape[1] // HEAD_DIM
    group = heads // kv_heads
    chunk = rows // chunks
    right = jnp.minimum(me + 1, n - 1)
    left = jnp.maximum(me - 1, 0)

    barrier = pltpu.get_barrier_semaphore()

    @pl.when(me > 0)
    def _():
        pl.semaphore_signal(barrier, inc=1, device_id={"cp": left}, device_id_type=MESH)

    def span(c):
        return pl.ds(pl.multiple_of(c * chunk, chunk), chunk)

    def key_part(slot, c):
        return k_buf.at[slot, span(c), :]

    def value_part(slot, c):
        return v_buf.at[slot, span(c), :]

    own_copies = [
        pltpu.make_async_copy(id_hbm, id_buf.at[0], own_sem.at[0]),
        pltpu.make_async_copy(k_hbm, k_buf.at[0], own_sem.at[1]),
        pltpu.make_async_copy(v_hbm, v_buf.at[0], own_sem.at[2]),
    ]

    def remote(piece, source, target, slot):
        return pltpu.make_async_remote_copy(
            src_ref=source,
            dst_ref=target,
            send_sem=send_sem.at[slot, piece],
            recv_sem=recv_sem.at[slot, piece],
            device_id={"cp": right},
            device_id_type=MESH,
        )

    def id_hop(slot):
        return remote(0, id_buf.at[slot], id_buf.at[slot + 1], slot)

    def key_hop(slot, c):
        return remote(1 + 2 * c, key_part(slot, c), key_part(slot + 1, c), slot)

    def value_hop(slot, c):
        return remote(2 + 2 * c, value_part(slot, c), value_part(slot + 1, c), slot)

    q_copies = [pltpu.make_async_copy(q_hbm, q_raw, q_sem.at[0]),
                pltpu.make_async_copy(local_hbm, local, q_sem.at[1]),
                pltpu.make_async_copy(base_hbm, base_ref, q_sem.at[2])]
    for copy in own_copies + q_copies:
        copy.start()
    for copy in own_copies:
        copy.wait()

    @pl.when(me < n - 1)
    def _():
        pl.semaphore_wait(barrier, 1)
        id_hop(0).start()
        for c in range(chunks):
            key_hop(0, c).start()
        for c in range(chunks):
            value_hop(0, c).start()

    def phases(block, start, size):
        row = base_ref[block]
        cb, sb = row[0:1, :], row[1:2, :]
        cr = local[0, pl.ds(start, size), :]
        sr = local[1, pl.ds(start, size), :]
        return cb * cr - sb * sr, sb * cr + cb * sr

    def turn(x, cosine, sine):
        x = x.astype(jnp.float32)
        return x * cosine + pltpu.roll(x, HEAD_DIM // 2, axis=1) * sine

    for copy in q_copies:
        copy.wait()
    cosine, sine = phases(me, 0, rows)
    scale = math.log2(math.e) / math.sqrt(HEAD_DIM)
    cosine, sine = cosine * scale, sine * scale
    for h in range(heads):
        x = turn(q_raw[:, h * HEAD_DIM:(h + 1) * HEAD_DIM], cosine, sine)
        q_turned[h] = x.T.astype(jnp.bfloat16)
    acc[...] = jnp.zeros_like(acc)
    total[...] = jnp.zeros_like(total)
    top[...] = jnp.full_like(top, HIDDEN)
    row_index = lax.broadcasted_iota(jnp.int32, (chunk, rows), 1)
    key_index = lax.broadcasted_iota(jnp.int32, (chunk, rows), 0)

    def weigh(k, c):
        @pl.when(k > 0)
        def _():
            @pl.when(c == 0)
            def _():
                id_hop(k - 1).wait_recv()

            key_hop(k - 1, c).wait_recv()

            @pl.when(me < n - 1)
            def _():
                @pl.when(c == 0)
                def _():
                    id_hop(k).start()

                key_hop(k, c).start()

        @pl.when(c == 0)
        def _():
            key_id = id_buf[k].astype(jnp.float32)
            id_column[...] = jnp.broadcast_to(key_id, (HEAD_DIM, rows)).T

        row_id = id_buf[0].astype(jnp.float32)
        key_id = id_column[span(c), :][:, :1]
        keep = (key_id == row_id) & (key_index + (c * chunk - k * rows) <= row_index)
        bias[...] = jnp.where(keep, 0.0, HIDDEN)
        cosine, sine = phases(me - k, pl.multiple_of(c * chunk, chunk), chunk)
        for g in range(kv_heads):
            lanes = slice(g * HEAD_DIM, (g + 1) * HEAD_DIM)
            key = turn(k_buf[k, span(c), lanes], cosine, sine).astype(jnp.bfloat16)
            for h in range(g * group, (g + 1) * group):
                scores = jnp.dot(key, q_turned[h], preferred_element_type=jnp.float32)
                scores = scores + bias[...]
                old = top[h:h + 1, :]
                new = jnp.maximum(old, jnp.max(scores, axis=0, keepdims=True))
                weight = jnp.exp2(scores - new)
                change = jnp.exp2(old - new)
                top[h:h + 1, :] = new
                factor[c, h:h + 1, :] = change
                total[h:h + 1, :] = total[h:h + 1, :] * change + jnp.sum(
                    weight, axis=0, keepdims=True
                )
                weights[c, h] = weight.astype(jnp.bfloat16)

    def arrive(k, c):
        @pl.when(k > 0)
        def _():
            value_hop(k - 1, c).wait_recv()

            @pl.when(me < n - 1)
            def _():
                value_hop(k, c).start()

    def gather(k, c):
        arrive(k, c)
        for g in range(kv_heads):
            lanes = slice(g * HEAD_DIM, (g + 1) * HEAD_DIM)
            value = v_buf[k, span(c), lanes].T
            for h in range(g * group, (g + 1) * group):
                acc[h] = acc[h] * factor[c, h:h + 1, :] + jnp.dot(
                    value, weights[c, h], preferred_element_type=jnp.float32
                )

    def step(t, unused):
        k, c = t // (2 * chunks), t % (2 * chunks)

        @pl.when(c < chunks)
        def _():
            weigh(k, c)

        @pl.when(c >= chunks)
        def _():
            gather(k, c - chunks)

        return unused

    lax.fori_loop(0, (me + 1) * 2 * chunks - 1, step, 0)
    arrive(me, chunks - 1)
    v_last[...] = v_buf[me, span(chunks - 1), :]

    @pl.when(me < n - 1)
    def _():
        def drain(k, unused):
            id_hop(k).wait_send()
            for c in range(chunks):
                key_hop(k, c).wait_send()
                value_hop(k, c).wait_send()
            return unused

        lax.fori_loop(0, me + 1, drain, 0)


def finish(acc, weights, factor, total, v_last, out_hbm, stage, sem):
    last, heads = weights.shape[0] - 1, acc.shape[0]
    kv_heads = v_last.shape[1] // HEAD_DIM
    group = heads // kv_heads
    burst = math.gcd(group, BURST)
    copies = []
    for h in range(heads):
        g = h // group
        if h % group == 0:
            value = v_last[:, g * HEAD_DIM:(g + 1) * HEAD_DIM].T
        result = acc[h] * factor[last, h:h + 1, :] + jnp.dot(
            value, weights[last, h], preferred_element_type=jnp.float32
        )
        result = result * (1.0 / total[h:h + 1, :])
        stage[:, h * HEAD_DIM:(h + 1) * HEAD_DIM] = result.T.astype(stage.dtype)
        if (h + 1) % burst == 0:
            lanes = pl.ds((h + 1 - burst) * HEAD_DIM, burst * HEAD_DIM)
            copies.append(pltpu.make_async_copy(
                stage.at[:, lanes], out_hbm.at[:, lanes], sem.at[len(copies)]
            ))
            copies[-1].start()
    for copy in copies:
        copy.wait()


def body(n, queries, keys, values, segment_ids):
    rows, width = queries.shape
    kv_width = keys.shape[1]
    heads = width // HEAD_DIM
    chunks = 2
    chunk = rows // chunks
    local, base = tables(rows, n)
    anywhere = pl.BlockSpec(memory_space=pltpu.HBM)
    vmem = pl.BlockSpec(memory_space=pltpu.VMEM)
    count = 1 + 2 * chunks
    operands = (queries, keys, values, segment_ids.reshape(1, rows),
                jnp.asarray(local), jnp.asarray(base))
    state = pl.pallas_call(
        functools.partial(attend, n, chunks),
        out_shape=[
            pltpu.VMEM((heads, HEAD_DIM, rows), jnp.float32),
            pltpu.VMEM((chunks, heads, chunk, rows), jnp.bfloat16),
            pltpu.VMEM((chunks, heads, rows), jnp.float32),
            pltpu.VMEM((heads, rows), jnp.float32),
            pltpu.VMEM((chunk, kv_width), values.dtype),
        ],
        in_specs=[anywhere] * 6,
        out_specs=[vmem] * 5,
        scratch_shapes=[
            pltpu.VMEM((rows, width), queries.dtype),
            pltpu.VMEM((heads, HEAD_DIM, rows), jnp.bfloat16),
            pltpu.VMEM((n, rows, kv_width), keys.dtype),
            pltpu.VMEM((n, rows, kv_width), values.dtype),
            pltpu.VMEM((n, 1, rows), jnp.int32),
            pltpu.VMEM((2, rows, HEAD_DIM), jnp.float32),
            pltpu.VMEM((n, 2, HEAD_DIM), jnp.float32),
            pltpu.VMEM((rows, HEAD_DIM), jnp.float32),
            pltpu.VMEM((chunk, rows), jnp.float32),
            pltpu.VMEM((heads, rows), jnp.float32),
            pltpu.SemaphoreType.DMA((3,)),
            pltpu.SemaphoreType.DMA((3,)),
            pltpu.SemaphoreType.DMA((max(n - 1, 1), count)),
            pltpu.SemaphoreType.DMA((max(n - 1, 1), count)),
        ],
        compiler_params=pltpu.CompilerParams(
            collective_id=0, has_side_effects=True, vmem_limit_bytes=VMEM_LIMIT
        ),
    )(*[pltpu.with_memory_space_constraint(x, pltpu.HBM) for x in operands])
    return pl.pallas_call(
        finish,
        out_shape=jax.ShapeDtypeStruct((rows, width), queries.dtype),
        in_specs=[vmem] * 5,
        out_specs=anywhere,
        scratch_shapes=[
            pltpu.VMEM((rows, width), queries.dtype),
            pltpu.SemaphoreType.DMA((heads,)),
        ],
        compiler_params=pltpu.CompilerParams(vmem_limit_bytes=VMEM_LIMIT),
    )(*state)


def solution(mesh):
    return jax.shard_map(
        functools.partial(body, mesh.shape["cp"]),
        mesh=mesh,
        in_specs=(
            P(("rep", "cp"), "tp"),
            P(("rep", "cp"), "tp"),
            P(("rep", "cp"), "tp"),
            P(("rep", "cp")),
        ),
        out_specs=P(("rep", "cp"), "tp"),
        check_vma=False,
    )
```
